32 devices in a mesh: expert: 8 (over z, x), width: 4 (over y, core).
Axes of the slice: x: 2, y: 2, z: 4, core: 2. Of those that a mesh axis runs over, the one named last changes fastest.
Arguments:
- tokens: bfloat16 [1024, 4096], P('expert'), may hold values from -6 to 6
- expert_ids: int32 [1024, 8], P('expert'), may hold values from 0 to 15, all different within a row; in each aligned block of 128 rows (0 to 127, 128 to 255, ...) at most 128 rows name the same one
- combine_weights: float32 [1024, 8], P('expert'), may hold values from 0.05 to 0.3
- gate_weight: bfloat16 [16, 4096, 1536], P('expert', None, 'width'), may hold values from -0.09375 to 0.09375
- up_weight: bfloat16 [16, 4096, 1536], P('expert', None, 'width'), may hold values from -0.09375 to 0.09375
- down_weight: bfloat16 [16, 1536, 4096], P('expert', 'width'), may hold values from -0.15625 to 0.15625
Outputs:
- mixed: bfloat16 [1024, 4096], P('expert', 'width')
The draws below stay inside these ranges and needn't reach their ends.
Inputs may be any that keep to these rules, and one draw needn't show every extreme that they name: `expert_ids`: each token names 8 different experts. Within the tokens of one index of expert (aligned blocks of 128 tokens) no expert is named by more than 128 tokens, a bound that some block reaches.
All inputs are finite; a program needn't handle non-finite values.
Results may differ from the reference program's by a relative error of at most 0.012.
Values may be sent and summed in bfloat16 or wider, within the bound.
A program may use at most 128 MiB of HBM per device.

```python
import math
import jax
import jax.numpy as jnp
import numpy as np
from jax import lax

D = 4096
FF = 1536
TOP = 8
TOK_DEV = 128
EXPERTS = 16
TOKENS = 1024
MOST = 128
N_EXPERT = 8
N_WIDTH = 4


def block_scale(key, extent, cuts, least, largest):
    loudness = 1.0
    for position, shards_of in cuts:
        steps = jax.random.uniform(jax.random.fold_in(jax.random.fold_in(key, 6), position), (shards_of,), jnp.float32, least / len(cuts), largest / len(cuts))
        loudness = loudness * jnp.repeat(jnp.exp(steps), extent[position] // shards_of).reshape((-1,) + (1,) * (len(extent) - 1 - position))
    return loudness


def deal_out(stream_key, own, number, rows, count, top, reach, slope):
    ranking = jax.random.permutation(stream_key, count)
    crowded, common = shares(count, rows * top, reach, slope, True), shares(count, rows * top, reach, slope, False)
    places = jnp.arange(count)

    def named(sizes, offset_by):
        used = int((sizes > 0).sum())
        fixed = max(1, used // 4)
        moved = fixed + (places - fixed + offset_by * (used - fixed)) % max(1, count - fixed)
        return jnp.zeros((count,), jnp.int32).at[ranking[jnp.where(places < fixed, places, moved)]].set(jnp.asarray(sizes, jnp.int32))

    sizes = jnp.where(number % 4 == 0, named(crowded, number // 4), named(common, number - number // 4 - 1))
    mixed = jax.random.permutation(jax.random.fold_in(own, 3), count)
    source_of, sink = mixed[0:count // 2 * 2:2], mixed[1:count // 2 * 2:2]
    room = jnp.minimum(sizes[source_of] - 1, reach - sizes[sink]) // 2
    room = jnp.where((source_of == ranking[0]) | (sink == ranking[0]) | (sizes[sink] == 0), 0, jnp.maximum(room, 0))
    moved = jax.random.randint(jax.random.fold_in(own, 4), (count // 2,), 0, 1 << 20) % (room + 1)
    sizes = sizes.at[source_of].add(-moved).at[sink].add(moved)
    members = jnp.searchsorted(jnp.cumsum(sizes), jnp.arange(rows * top), side="right").astype(jnp.int32)
    listing = members.reshape(top, rows).T
    listing = listing[jax.random.permutation(jax.random.fold_in(own, 1), rows)]
    offset_by = jax.random.randint(jax.random.fold_in(own, 2), (rows, 1), 0, top)
    return jnp.take_along_axis(listing, (jnp.arange(top)[None, :] + offset_by) % top, axis=1)


def shares(number_of, total, bound, skew, full):
    portions = [(1 << 20) // math.isqrt(grade ** skew) + 1 for grade in range(1, number_of + 1)]
    largest = bound if full else min(bound, max(-(-total // number_of), total * portions[0] // sum(portions)))
    least = 1 if total - largest >= number_of - 1 else 0
    given, spare = [largest] + [least] * (number_of - 1), total - largest - least * (number_of - 1)
    while spare > 0:
        movable = [i for i in range(1, number_of) if given[i] < largest] or [i for i in range(1, number_of) if given[i] < bound]
        pool, remaining = sum([portions[i] for i in movable]), spare
        for i in movable:
            addition = min(bound - given[i], max(1, remaining * portions[i] // pool), spare)
            given[i] = given[i] + addition
            spare = spare - addition
    return np.array(given)


def scatter_about(own_key, shape, deviation, limit, pieces=(), kind=jnp.bfloat16):
    result = jax.random.normal(own_key, shape, jnp.float32) * deviation
    if len(pieces) > 0:
        result = block_scale(own_key, shape, pieces, -0.22, 0.18) * result
    return jnp.clip(result, min=-limit, max=limit).astype(kind)


def setup_inputs(seed: int = 0) -> dict:
    key_list = jax.random.split(jax.random.key(seed), 7)
    tokens = scatter_about(key_list[0], (TOKENS, D), 1.0, 6.0, ((0, 8),))
    expert_ids_keys = jax.random.split(jax.random.fold_in(key_list[1], 1), TOKENS // TOK_DEV)
    expert_ids_turns = jax.random.permutation(jax.random.fold_in(key_list[1], 3), TOKENS // TOK_DEV)
    expert_ids = jax.vmap(lambda own, number: deal_out(jax.random.fold_in(key_list[1], 2), own, number, TOK_DEV, EXPERTS, TOP, MOST, 1))(expert_ids_keys, expert_ids_turns).reshape((TOKENS, TOP))
    combine_weights = jnp.clip(0.05 + 0.25 * jax.random.uniform(key_list[2], (TOKENS, TOP), jnp.float32) ** block_scale(key_list[2], (TOKENS, TOP), ((0, 8),), -0.2, 0.2), 0.05, 0.3)
    gate_weight = scatter_about(key_list[3], (EXPERTS, D, FF), D ** -0.5, 0.09375, ((0, 8), (2, 4)))
    up_weight = scatter_about(key_list[4], (EXPERTS, D, FF), D ** -0.5, 0.09375, ((0, 8), (2, 4)))
    down_weight = scatter_about(key_list[5], (EXPERTS, FF, D), FF ** -0.5, 0.15625, ((0, 8), (1, 4)))
    return dict(tokens=tokens, expert_ids=expert_ids, combine_weights=combine_weights, gate_weight=gate_weight, up_weight=up_weight, down_weight=down_weight)


def ranks_of(expert_ids):
    flat_ids = expert_ids.reshape(N_EXPERT, TOK_DEV * TOP)
    onehot = (flat_ids[:, :, None] == jnp.arange(EXPERTS, dtype=jnp.int32)[None, None, :]).astype(jnp.int32)
    counted = jnp.cumsum(onehot, axis=1)
    return jnp.sum(counted * onehot, axis=2).astype(jnp.int32) - 1


def reference(tokens, expert_ids, combine_weights, gate_weight, up_weight, down_weight):
    rank = ranks_of(expert_ids)
    flat_ids = expert_ids.reshape(N_EXPERT, TOK_DEV * TOP)
    source = jnp.arange(N_EXPERT, dtype=jnp.int32)[:, None]
    slot = flat_ids * (N_EXPERT * MOST) + source * MOST + rank
    token_index = source * TOK_DEV + jnp.arange(TOK_DEV * TOP, dtype=jnp.int32)[None, :] // TOP
    table = jnp.full((EXPERTS * N_EXPERT * MOST,), TOKENS, jnp.int32)
    table = table.at[slot.reshape(-1)].set(token_index.reshape(-1))
    padded = jnp.concatenate([tokens, jnp.zeros((1, D), jnp.bfloat16)], axis=0)
    group = FF // N_WIDTH

    def one_expert(packed):
        gate_one, up_one, down_one, rows_index = packed
        rows = padded[rows_index]
        total = jnp.zeros((rows.shape[0], D), jnp.float32)
        for index in range(N_WIDTH):
            gate = jnp.dot(rows, gate_one[:, index * group:(index + 1) * group], preferred_element_type=jnp.float32)
            up = jnp.dot(rows, up_one[:, index * group:(index + 1) * group], preferred_element_type=jnp.float32)
            hidden = (jax.nn.silu(gate) * up).astype(jnp.bfloat16)
            partial_value = jnp.dot(hidden, down_one[index * group:(index + 1) * group, :], preferred_element_type=jnp.float32)
            total = total + partial_value.astype(jnp.bfloat16).astype(jnp.float32)
        return total

    outputs = lax.map(one_expert, (gate_weight, up_weight, down_weight, table.reshape(EXPERTS, N_EXPERT * MOST)))
    outputs = outputs.reshape(EXPERTS * N_EXPERT * MOST, D)
    slot_tokens = slot.reshape(TOKENS, TOP)
    mixed = jnp.zeros((TOKENS, D), jnp.float32)
    for choice_index in range(TOP):
        mixed = mixed + combine_weights[:, choice_index:choice_index + 1] * outputs[slot_tokens[:, choice_index]]
    return mixed.astype(jnp.bfloat16)
```

```python
import functools

import jax
import jax.numpy as jnp
from jax import lax
from jax.experimental import pallas as pl
from jax.experimental.pallas import tpu as pltpu
from jax.sharding import PartitionSpec as P

LANE = 128
SUB = 8
F32 = jnp.float32
BF16 = jnp.bfloat16
MESH = pl.DeviceIdType.MESH


def kernel(nz, resident, exp_local, rows, width_all, ff,
           x_ref, ids_ref, wts_ref, g_hbm, u_hbm, d_hbm, out_ref, *rest):
    if resident:
        land, rest = rest[-1], rest[:-1]
        xbuf = lsem = None
    else:
        land, rest = rest[0], rest[1:]
        xbuf, lsem, rest = rest[-2], rest[-1], rest[:-2]
    (wgu, dwv, acc, hid, hidr, part, yr2, xr2, x3s, y3s, x3r, y3r, zsb, zr4, own, cwt, cw,
     wsem, osem, snd, xr, yr, zr, cr, cwr, dwr, hr, r2r, r3r, z4r) = rest

    e, w = lax.axis_index("expert"), lax.axis_index("width")
    z, x = e // 2, e % 2
    y, c = w // 2, w % 2
    s = (x + y) % 2
    n_expert = 2 * nz
    deep = exp_local * ff
    cols = width_all // 4
    half = cols // 2
    quarter = rows // 4
    xdev = (z * 2 + 1 - x, w)
    ydev = (e, (1 - y) * 2 + c)
    cdev = (e, y * 2 + 1 - c)

    def plane_dev(plane):
        return plane * 2 + x, w

    def remote(src, dst, send, recv, dev):
        return pltpu.make_async_remote_copy(
            src_ref=src, dst_ref=dst, send_sem=send, recv_sem=recv,
            device_id=dev, device_id_type=MESH)

    sites = [0]
    pending = []

    def go(src, dst, recv, dev, cond=None, keep=True):
        copy = remote(src, dst, snd.at[sites[0]], recv, dev)
        sites[0] += 1
        if cond is None:
            copy.start()
        else:
            pl.when(cond)(copy.start)
        if keep:
            pending.append((copy, cond))
        return copy

    def arrived(ref, recv):
        remote(ref, ref, snd.at[0], recv, xdev).wait_recv()

    def piece(cls, core):
        return pl.ds(pl.multiple_of((cls * 2 + core) * quarter, quarter), quarter)

    mine, twin = piece(s, c), piece(1 - s, c)
    core_mine, core_twin = piece(s, 1 - c), piece(1 - s, 1 - c)

    def block(plane, j):
        return plane * 2 + (x if j == 0 else 1 - x)

    barrier = pltpu.get_barrier_semaphore()
    for q in range(1, n_expert):
        pl.semaphore_signal(barrier, inc=1, device_id=((e + q) % n_expert, w), device_id_type=MESH)
    for peer in (ydev, cdev):
        pl.semaphore_signal(barrier, inc=1, device_id=peer, device_id_type=MESH)
    pl.semaphore_wait(barrier, n_expert + 1)

    go(x_ref.at[twin], land.at[e, twin], xr.at[z], xdev)
    for sign in (1, -1):
        go(x_ref.at[mine], land.at[e, mine], zr.at[z, 0], plane_dev(z + sign),
           (z + sign >= 0) & (z + sign < nz))
    own_load = pltpu.make_async_copy(x_ref, land.at[e], osem)
    own_load.start()

    weights = []
    for k in range(exp_local):
        for i, ref in enumerate((g_hbm, u_hbm)):
            copy = pltpu.make_async_copy(
                ref.at[k], wgu.at[k, :, i * ff:(i + 1) * ff], wsem.at[2 * k + i])
            copy.start()
            weights.append(copy)

    def spans(core):
        first = pl.multiple_of((2 * y + core) * cols, LANE)
        second = pl.multiple_of((2 * (1 - y) + core) * cols, LANE)
        return ((pl.ds(first, cols), slice(0, cols)),
                (pl.ds(pl.multiple_of(second + half, LANE), half), slice(cols, cols + half)),
                (pl.ds(second, half), slice(cols + half, 2 * cols)))

    downs = []
    for i, (src, dst) in enumerate(spans(c)):
        copy = pltpu.make_async_copy(d_hbm.at[:, src], dwv.at[0, :, dst], wsem.at[2 * exp_local + i])
        copy.start()
        downs.append(copy)
    for i, (src, dst) in enumerate(spans(1 - c)):
        go(d_hbm.at[:, src], dwv.at[1, :, dst], dwr.at[i], cdev)

    lanes = cwt.shape[0] * SUB
    lane = lax.broadcasted_iota(jnp.int32, (rows, lanes), 1)
    spot = lane % SUB
    name = jnp.where(spot < exp_local, (lane // SUB) * exp_local + spot, -1)
    dense = jnp.zeros((rows, lanes), F32)
    for k in range(ids_ref.shape[1]):
        dense = dense + jnp.where(ids_ref[:, k:k + 1] == name, wts_ref[:, k:k + 1], 0.0)
    for i in range(lanes // LANE):
        turned = jnp.transpose(dense[:, i * LANE:(i + 1) * LANE])
        cwt[i * (LANE // SUB):(i + 1) * (LANE // SUB)] = turned.reshape(LANE // SUB, SUB, rows)
    for q in range(1, n_expert):
        to = (e + q) % n_expert
        go(cwt.at[to], cw.at[e], cwr.at[e], (to, w))
    cw[e] = cwt[e]

    def order(k):
        if k == 0:
            return z
        short = jnp.minimum(z, nz - 1 - z)
        way = jnp.where(2 * z < nz - 1, 1, -1)
        near = (k + 1) // 2 if k % 2 else -(k // 2)
        return z + way * jnp.where(k <= 2 * short, near, k - short)

    planes = [order(k) for k in range(nz)]

    def take_x0():
        ref = land.at[block(z, 1), mine]
        arrived(ref, xr.at[z])
        for sign in (1, -1):
            go(ref, ref, zr.at[z, 1], plane_dev(z + sign), (z + sign >= 0) & (z + sign < nz))
        go(ref, ref, yr.at[z], ydev)
        go(ref, ref, cr.at[z, 1], cdev)

    def take_y0():
        ref = land.at[block(z, 1), twin]
        arrived(ref, yr.at[z])
        go(ref, ref, cr.at[z, 3], cdev)

    def take_z(d, j):
        for sign in (1, -1):
            plane, onward = z + sign * d, z - sign
            here = (plane >= 0) & (plane < nz)
            further = here & (onward >= 0) & (onward < nz)
            ref = land.at[block(plane, j), mine]

            @pl.when(here)
            def _():
                arrived(ref, zr.at[plane, j])

            go(ref, ref, zr.at[plane, j], plane_dev(onward), further)
            if j == 0:
                go(ref, ref, xr.at[plane], xdev, here)
                go(ref, ref, yr.at[plane], ydev, here)
            go(ref, ref, cr.at[plane, j], cdev, here)

    def take_xy(k):
        plane = planes[k]
        ref = land.at[block(plane, 0), twin]
        arrived(ref, yr.at[plane])
        go(ref, ref, cr.at[plane, 2], cdev)
        ref = land.at[block(plane, 1), twin]
        arrived(ref, xr.at[plane])
        go(ref, ref, cr.at[plane, 3], cdev)

    def load_pair(k):
        if not resident:
            pair = pl.ds(2 * planes[k], 2)
            copy = pltpu.make_async_copy(land.at[pair], xbuf.at[k % 2], lsem)
            copy.start()
            copy.wait()

    def take_c(k):
        plane = planes[k]
        for i in range(4):
            if k == 0 and i % 2 == 0:
                continue
            ref = land.at[block(plane, i % 2), core_mine if i < 2 else core_twin]
            arrived(ref, cr.at[plane, i])
        for j in range(2):
            if k or j:
                ref = cw.at[block(plane, j)]
                arrived(ref, cwr.at[block(plane, j)])
        load_pair(k)

    hid_sends, sends2, sends3, sends4 = {}, {}, {}, {}
    tile = 256

    def up(k):
        slot = k % 2
        pair = (land.at[pl.ds(2 * planes[k], 2)] if resident else xbuf.at[k % 2])
        if k >= 2:
            for copy in hid_sends[k - 2]:
                copy.wait_send()
        hid_sends[k] = []
        square = (rows, rows)
        eye = lax.broadcasted_iota(jnp.int32, square, 0) == lax.broadcasted_iota(jnp.int32, square, 1)
        for j in range(exp_local):
            if k == 0:
                weights[2 * j].wait()
                weights[2 * j + 1].wait()
            def gate_up(at):
                acc[:, at] = jnp.dot(pair[...].reshape(2 * rows, width_all), wgu[j, :, at],
                                     preferred_element_type=F32)

            if resident:
                for i in range(2 * ff // tile):
                    gate_up(slice(i * tile, (i + 1) * tile))
            else:
                @pl.loop(0, 2 * ff // tile)
                def _(i):
                    gate_up(pl.ds(pl.multiple_of(i * tile, LANE), tile))

            for b in range(2):
                row = cw[2 * planes[k] + b, j:j + 1, :]
                scale = jnp.sum(jnp.where(eye, jnp.broadcast_to(row, square), 0.0), axis=1, keepdims=True)
                band = slice(b * rows, (b + 1) * rows)
                gate, upp = acc[band, 0:ff], acc[band, ff:2 * ff]
                hid[slot, band, j * ff:(j + 1) * ff] = (jax.nn.silu(gate) * upp * scale).astype(BF16)
            at = slice(j * ff, (j + 1) * ff)
            hid_sends[k].append(go(hid.at[slot, :, at], hidr.at[k, :, at], hr.at[k, j], cdev, keep=k >= nz - 2))

    def down(k):
        slot = k % 2
        if k == 0:
            for copy in downs:
                copy.wait()
            for i, (_, dst) in enumerate(spans(c)):
                arrived(dwv.at[1, :, dst], dwr.at[i])
        if k >= 2:
            for copy in sends2[k - 2]:
                copy.wait_send()
        for j in range(exp_local):
            at = slice(j * ff, (j + 1) * ff)
            arrived(hidr.at[k, :, at], hr.at[k, j])

        def product(i):
            at = slice(i * half, (i + 1) * half)
            value = (jnp.dot(hid[slot], dwv[0, :, at], preferred_element_type=F32)
                     + jnp.dot(hidr[k], dwv[1, :, at], preferred_element_type=F32))
            part[slot, :, :, at] = value.astype(BF16).reshape(2, rows, half)

        last = k >= nz - 2
        sends2[k] = []
        product(3)
        sends2[k].append(go(part.at[slot, :, :, 3 * half:4 * half], yr2.at[k], r2r.at[k, 0], ydev, keep=last))
        product(1)
        product(2)
        sends2[k].append(go(part.at[slot, 1 - x, :, half:3 * half], xr2.at[k], r2r.at[k, 1], xdev, keep=last))
        product(0)

    def reduce2(k):
        slot = k % 2
        if k >= 2:
            for copy in sends3[k - 2]:
                copy.wait_send()
        last = k >= nz - 2
        sends3[k] = []
        arrived(yr2.at[k], r2r.at[k, 0])
        x3s[slot] = (part[slot, 1 - x, :, 0:half].astype(F32) + yr2[k, 1 - x].astype(F32)).astype(BF16)
        sends3[k].append(go(x3s.at[slot], x3r.at[k], r3r.at[k, 0], xdev, keep=last))
        arrived(xr2.at[k], r2r.at[k, 1])
        y3s[slot] = (part[slot, x, :, 2 * half:3 * half].astype(F32) + xr2[k, :, half:cols].astype(F32)).astype(BF16)
        sends3[k].append(go(y3s.at[slot], y3r.at[k], r3r.at[k, 1], ydev, keep=last))

    def reduce3(k):
        slot = k % 2
        if k >= 3:
            sends4[k - 2].wait_send()
        arrived(x3r.at[k], r3r.at[k, 0])
        arrived(y3r.at[k], r3r.at[k, 1])
        left = part[slot, x, :, 0:half].astype(F32) + yr2[k, x].astype(F32) + x3r[k].astype(F32)
        right = part[slot, x, :, half:cols].astype(F32) + xr2[k, :, 0:half].astype(F32) + y3r[k].astype(F32)
        if k == 0:
            own[:, 0:half] = left
            own[:, half:cols] = right
        else:
            zsb[slot, :, 0:half] = left.astype(BF16)
            zsb[slot, :, half:cols] = right.astype(BF16)
            sends4[k] = go(zsb.at[slot], zr4.at[z], z4r.at[z], plane_dev(planes[k]), keep=k >= nz - 2)

    take_x0()
    if nz > 1:
        take_z(1, 0)
    take_y0()
    if nz > 1:
        take_z(1, 1)
    own_load.wait()
    take_c(0)
    for k in range(nz):
        if k:
            take_xy(k)
            if k >= 2:
                take_z(k, 1)
            take_c(k)
        up(k)
        if 2 <= k < nz - 1:
            take_z(k + 1, 0)
        if k >= 2:
            reduce3(k - 2)
        down(k)
        if k >= 1:
            reduce2(k - 1)
        if k == 0 and nz > 2:
            take_z(2, 0)
    if nz >= 2:
        reduce3(nz - 2)
    reduce2(nz - 1)
    reduce3(nz - 1)
    total = own[...]
    for q in range(1, nz):
        plane = (z + q) % nz
        arrived(zr4.at[plane], z4r.at[plane])
        total = total + zr4[plane].astype(F32)
    out_ref[...] = total.astype(BF16)
    for copy, cond in pending:
        if cond is None:
            copy.wait_send()
        else:
            pl.when(cond)(copy.wait_send)
    assert sites[0] <= snd.shape[0]


def local(tokens, expert_ids, combine_weights, gate_weight, up_weight, down_weight):
    rows, width_all = tokens.shape
    exp_local, _, ff = gate_weight.shape
    n_expert = lax.axis_size("expert")
    n_width = lax.axis_size("width")
    assert n_width == 4 and n_expert % 2 == 0 and rows == LANE and exp_local <= SUB
    nz = n_expert // 2
    cols = width_all // n_width
    half = cols // 2
    deep = exp_local * ff
    lanes = -(-n_expert * SUB // LANE) * LANE
    resident = n_expert * rows * width_all * 2 <= 12 * 2**20
    dma = pltpu.SemaphoreType.DMA
    anyspace = pl.BlockSpec(memory_space=pl.ANY)
    vmem = pl.BlockSpec(memory_space=pltpu.VMEM)
    out_shape = [jax.ShapeDtypeStruct((rows, cols), BF16)]
    out_specs = [vmem]
    scratch = [
        pltpu.VMEM((exp_local, width_all, 2 * ff), BF16),
        pltpu.VMEM((2, deep, 2 * cols), BF16),
        pltpu.VMEM((2 * rows, 2 * ff), F32),
        pltpu.VMEM((2, 2 * rows, deep), BF16),
        pltpu.VMEM((nz, 2 * rows, deep), BF16),
        pltpu.VMEM((2, 2, rows, 2 * cols), BF16),
        pltpu.VMEM((nz, 2, rows, half), BF16),
        pltpu.VMEM((nz, rows, cols), BF16),
        pltpu.VMEM((2, rows, half), BF16),
        pltpu.VMEM((2, rows, half), BF16),
        pltpu.VMEM((nz, rows, half), BF16),
        pltpu.VMEM((nz, rows, half), BF16),
        pltpu.VMEM((2, rows, cols), BF16),
        pltpu.VMEM((nz, rows, cols), BF16),
        pltpu.VMEM((rows, cols), F32),
        pltpu.VMEM((lanes // SUB, SUB, rows), F32),
        pltpu.VMEM((n_expert, SUB, rows), F32),
        dma((2 * exp_local + 3,)),
        dma,
        dma((32 * nz + 16,)),
        dma((nz,)), dma((nz,)), dma((nz, 2)), dma((nz, 4)), dma((n_expert,)),
        dma((3,)), dma((nz, exp_local)), dma((nz, 2)), dma((nz, 2)), dma((nz,)),
    ]
    blocks = (n_expert, rows, width_all)
    if resident:
        scratch.append(pltpu.VMEM(blocks, BF16))
    else:
        out_shape.append(jax.ShapeDtypeStruct(blocks, BF16))
        out_specs.append(anyspace)
        scratch += [pltpu.VMEM((2, 2, rows, width_all), BF16), dma]
    out = pl.pallas_call(
        functools.partial(kernel, nz, resident, exp_local, rows, width_all, ff),
        out_shape=out_shape,
        in_specs=[anyspace, vmem, vmem, anyspace, anyspace, anyspace],
        out_specs=out_specs,
        scratch_shapes=scratch,
        compiler_params=pltpu.CompilerParams(
            collective_id=0, has_side_effects=True, vmem_limit_bytes=66_000_000),
    )(tokens, expert_ids, combine_weights, gate_weight, up_weight,
      down_weight.reshape(deep, width_all))
    return out[0]


def solution(mesh):
    placed = (
        P("expert", None),
        P("expert", None),
        P("expert", None),
        P("expert", None, "width"),
        P("expert", None, "width"),
        P("expert", "width", None),
    )
    return jax.shard_map(
        local, mesh=mesh, in_specs=placed, out_specs=P("expert", "width"), check_vma=False
    )
```

```python
import functools

import jax
import jax.numpy as jnp
from jax import lax
from jax.experimental import pallas as pl
from jax.experimental.pallas import tpu as pltpu
from jax.sharding import PartitionSpec as P

LANE = 128
SUB = 8
F32 = jnp.float32
BF16 = jnp.bfloat16
MESH = pl.DeviceIdType.MESH


def schedule(nz, slots):
    if nz == 4:
        return [('x0',), ('c', 0, 0), ('z', 1, 0, 1), ('z', 1, 1, 1), ('z', 1, 0, -1), ('xk', 1), ('yk', 1), ('z', 1, 1, -1), ('z', 2, 0, 1), ('c', 1, 1), ('y0',), ('U', 1, 1), ('c', 0, 1), ('c', 1, 0), ('D', 1, 1, 0), ('z', 2, 0, -1), ('D', 1, 1, 1), ('yk', 2), ('z', 3, 0, 1), ('xk', 2), ('U', 0, 1), ('c', 2, 0), ('z', 2, 1, 1), ('z', 3, 0, -1), ('z', 2, 1, -1), ('c', 2, 1), ('U', 2, 1), ('D', 0, 1, 0), ('U', 1, 0), ('D', 2, 1, 0), ('yk', 3), ('z', 3, 1, -1), ('D', 2, 1, 1), ('D', 1, 0, 0), ('U', 2, 0), ('c', 3, 0), ('z', 3, 1, 1), ('R2x', 1), ('xk', 3), ('U', 0, 0), ('c', 3, 1), ('D', 2, 0, 0), ('D', 1, 0, 1), ('R2y', 1), ('R2x', 2), ('U', 3, 1), ('D', 3, 1, 0), ('D', 3, 1, 1), ('R3l', 1), ('D', 2, 0, 1), ('R3l', 2), ('R2y', 2), ('U', 3, 0), ('R2x', 3), ('R3r', 1), ('D', 3, 0, 0), ('R3r', 2), ('D', 0, 1, 1), ('D', 3, 0, 1), ('R2y', 3), ('R3l', 3), ('D', 0, 0, 0), ('D', 0, 0, 1), ('R3r', 3), ('R2x', 0), ('R2y', 0), ('R3l', 0), ('R3r', 0)]
    def near(d, j):
        return [("z", d, j, 1), ("z", d, j, -1)] if d < nz else []

    order = [("x0",), *near(1, 0), ("y0",), *near(1, 1)]
    for k in range(nz):
        if k:
            order += [("xk", k), ("yk", k)]
        order += [("c", k, 1), ("U", k, 1), ("c", k, 0), ("U", k, 0), *near(k + 2, 0)]
        if k >= 2:
            order += [("R3l", k - 2), ("R3r", k - 2)]
        order += [("D", k, 1, 0), ("D", k, 1, 1), ("D", k, 0, 0), ("D", k, 0, 1), *near(k + 2, 1)]
        if k >= 1:
            order += [("R2x", k - 1), ("R2y", k - 1)]
    order += [("R2x", nz - 1), ("R2y", nz - 1)]
    for k in range(max(nz - 2, 0), nz):
        order += [("R3l", k), ("R3r", k)]
    return order


def kernel(nz, resident, slots, exp_local, rows, width_all, ff,
           x_ref, ids_ref, wts_ref, g_hbm, u_hbm, d_hbm, out_ref, *rest):
    if resident:
        land, rest = rest[-1], rest[:-1]
        xbuf = lsem = None
    else:
        land, rest = rest[0], rest[1:]
        xbuf, lsem, rest = rest[-2], rest[-1], rest[:-2]
    (wgu, dwv, acc, hid, hidr, part, yr2, xr2, x3s, y3s, x3r, y3r, zsb, zr4, own, cwt, cw,
     wsem, osem, snd, xr, yr, zr, cr, cwr, dwr, hr, r2r, r3r, z4r) = rest

    e, w = lax.axis_index("expert"), lax.axis_index("width")
    z, x = e // 2, e % 2
    y, c = w // 2, w % 2
    s = (x + y) % 2
    n_expert = 2 * nz
    deep = exp_local * ff
    cols = width_all // 4
    half = cols // 2
    quarter = rows // 4
    xdev = (z * 2 + 1 - x, w)
    ydev = (e, (1 - y) * 2 + c)
    cdev = (e, y * 2 + 1 - c)

    def plane_dev(plane):
        return plane * 2 + x, w

    def remote(src, dst, send, recv, dev):
        return pltpu.make_async_remote_copy(
            src_ref=src, dst_ref=dst, send_sem=send, recv_sem=recv,
            device_id=dev, device_id_type=MESH)

    sites = [0]
    pending = []

    def go(src, dst, recv, dev, cond=None, keep=True):
        copy = remote(src, dst, snd.at[sites[0]], recv, dev)
        sites[0] += 1
        if cond is None:
            copy.start()
        else:
            pl.when(cond)(copy.start)
        if keep:
            pending.append((copy, cond))
        return copy

    def arrived(ref, recv):
        remote(ref, ref, snd.at[0], recv, xdev).wait_recv()

    def piece(cls, core):
        return pl.ds(pl.multiple_of((cls * 2 + core) * quarter, quarter), quarter)

    mine, twin = piece(s, c), piece(1 - s, c)
    core_mine, core_twin = piece(s, 1 - c), piece(1 - s, 1 - c)

    def block(plane, j):
        return plane * 2 + (x if j == 0 else 1 - x)

    barrier = pltpu.get_barrier_semaphore()
    for q in range(1, n_expert):
        pl.semaphore_signal(barrier, inc=1, device_id=((e + q) % n_expert, w), device_id_type=MESH)
    for peer in (ydev, cdev):
        pl.semaphore_signal(barrier, inc=1, device_id=peer, device_id_type=MESH)
    pl.semaphore_wait(barrier, n_expert + 1)

    go(x_ref.at[twin], land.at[e, twin], xr.at[z], xdev)
    for sign in (1, -1):
        go(x_ref.at[mine], land.at[e, mine], zr.at[z, 0], plane_dev(z + sign),
           (z + sign >= 0) & (z + sign < nz))
    own_load = pltpu.make_async_copy(x_ref, land.at[e], osem)
    own_load.start()

    weights = []
    for k in range(exp_local):
        for i, ref in enumerate((g_hbm, u_hbm)):
            copy = pltpu.make_async_copy(
                ref.at[k], wgu.at[k, :, i * ff:(i + 1) * ff], wsem.at[2 * k + i])
            copy.start()
            weights.append(copy)

    def spans(core):
        first = pl.multiple_of((2 * y + core) * cols, LANE)
        second = pl.multiple_of((2 * (1 - y) + core) * cols, LANE)
        return ((pl.ds(first, cols), slice(0, cols)),
                (pl.ds(pl.multiple_of(second + half, LANE), half), slice(cols, cols + half)),
                (pl.ds(second, half), slice(cols + half, 2 * cols)))

    downs = []
    for i, (src, dst) in enumerate(spans(c)):
        copy = pltpu.make_async_copy(d_hbm.at[:, src], dwv.at[0, :, dst], wsem.at[2 * exp_local + i])
        copy.start()
        downs.append(copy)
    for i, (src, dst) in enumerate(spans(1 - c)):
        go(d_hbm.at[:, src], dwv.at[1, :, dst], dwr.at[i], cdev)

    tall = (n_expert * SUB, rows)
    line = lax.broadcasted_iota(jnp.int32, tall, 0)
    spot = line % SUB
    name = jnp.where(spot < exp_local, (line // SUB) * exp_local + spot, -1)
    dense = jnp.zeros(tall, F32)
    for k in range(ids_ref.shape[0]):
        dense = dense + jnp.where(ids_ref[k:k + 1, :] == name, wts_ref[k:k + 1, :], 0.0)
    cwt[...] = dense.reshape(n_expert, SUB, rows)
    for q in range(1, n_expert):
        to = (e + q) % n_expert
        go(cwt.at[to], cw.at[e], cwr.at[e], (to, w))
    cw[e] = cwt[e]

    def order(k):
        if k == 0:
            return z
        short = jnp.minimum(z, nz - 1 - z)
        way = jnp.where(2 * z < nz - 1, 1, -1)
        near = (k + 1) // 2 if k % 2 else -(k // 2)
        return z + way * jnp.where(k <= 2 * short, near, k - short)

    planes = [order(k) for k in range(nz)]

    def take_x0():
        ref = land.at[block(z, 1), mine]
        arrived(ref, xr.at[z])
        for sign in (1, -1):
            go(ref, ref, zr.at[z, 1], plane_dev(z + sign), (z + sign >= 0) & (z + sign < nz))
        go(ref, ref, yr.at[z], ydev)
        go(ref, ref, cr.at[z, 1], cdev)

    def take_y0():
        ref = land.at[block(z, 1), twin]
        arrived(ref, yr.at[z])
        go(ref, ref, cr.at[z, 3], cdev)

    def send_far(j):
        ref = x_ref.at[mine] if j == 0 else land.at[block(z, 1), mine]
        go(ref, land.at[block(z, j), mine], zr.at[z, j], plane_dev(nz - 1 - z), (z == 0) | (z == nz - 1))

    def take_z(d, j, side):
        sign = side * jnp.where(2 * z < nz - 1, 1, -1)
        plane, onward = z + sign * d, z - sign
        here = (plane >= 0) & (plane < nz)
        further = here & (onward >= 0) & (onward < nz)
        ref = land.at[block(plane, j), mine]

        @pl.when(here)
        def _():
            arrived(ref, zr.at[plane, j])

        if not far or d + 1 < nz - 1:
            go(ref, ref, zr.at[plane, j], plane_dev(onward), further)
        if j == 0:
            go(ref, ref, xr.at[plane], xdev, here)
            go(ref, ref, yr.at[plane], ydev, here)
        go(ref, ref, cr.at[plane, j], cdev, here)

    def take_x(k):
        plane = planes[k]
        ref = land.at[block(plane, 1), twin]
        arrived(ref, xr.at[plane])
        go(ref, ref, cr.at[plane, 3], cdev)

    def take_y(k):
        plane = planes[k]
        ref = land.at[block(plane, 0), twin]
        arrived(ref, yr.at[plane])
        go(ref, ref, cr.at[plane, 2], cdev)

    def take_c(k, j):
        whole = block(planes[k], j)
        if k == 0 and j == 0:
            own_load.wait()
        else:
            for i in (j, j + 2):
                arrived(land.at[whole, core_mine if i < 2 else core_twin], cr.at[planes[k], i])
            arrived(cw.at[whole], cwr.at[whole])
        if not resident:
            copy = pltpu.make_async_copy(land.at[whole], xbuf.at[k % 2, j], lsem)
            copy.start()
            copy.wait()

    sent = {}

    def put(key, k, src, dst, recv, dev):
        sent[key + (k,)] = go(src, dst, recv, dev, keep=k >= nz - slots)

    def reuse(key, k):
        if k >= slots:
            sent[key + (k - slots,)].wait_send()

    tile = 256
    first = []

    def up(k, j):
        if not first:
            for copy in weights:
                copy.wait()
            first.append(k)
        slot = k % slots
        tokens = (land.at[block(planes[k], j)] if resident else xbuf.at[k % 2, j])
        square = (rows, rows)
        eye = lax.broadcasted_iota(jnp.int32, square, 0) == lax.broadcasted_iota(jnp.int32, square, 1)
        for i in range(exp_local):
            def gate_up(at):
                acc[:, at] = jnp.dot(tokens[...], wgu[i, :, at], preferred_element_type=F32)

            if resident:
                for t in range(2 * ff // tile):
                    gate_up(slice(t * tile, (t + 1) * tile))
            else:
                @pl.loop(0, 2 * ff // tile)
                def _(t):
                    gate_up(pl.ds(pl.multiple_of(t * tile, LANE), tile))

            row = cw[block(planes[k], j), i:i + 1, :]
            scale = jnp.sum(jnp.where(eye, jnp.broadcast_to(row, square), 0.0), axis=1, keepdims=True)
            at = slice(i * ff, (i + 1) * ff)
            reuse(("h", j, i), k)
            hid[slot, j, :, at] = (jax.nn.silu(acc[:, 0:ff]) * acc[:, ff:2 * ff] * scale).astype(BF16)
            put(("h", j, i), k, hid.at[slot, j, :, at], hidr.at[k, j, :, at], hr.at[k, j, i], cdev)

    ready = []

    def product(k, j, i):
        at = slice(i * half, (i + 1) * half)
        value = (jnp.dot(hid[k % slots, j], dwv[0, :, at], preferred_element_type=F32)
                 + jnp.dot(hidr[k, j], dwv[1, :, at], preferred_element_type=F32))
        part[k % slots, j, :, at] = value.astype(BF16)

    def down(k, j, step):
        slot = k % slots
        if step == 0:
            if not ready:
                for copy in downs:
                    copy.wait()
                for i, (_, dst) in enumerate(spans(c)):
                    arrived(dwv.at[1, :, dst], dwr.at[i])
                ready.append(k)
            for i in range(exp_local):
                at = slice(i * ff, (i + 1) * ff)
                arrived(hidr.at[k, j, :, at], hr.at[k, j, i])
            reuse(("y2", j), k)
            product(k, j, 3)
            put(("y2", j), k, part.at[slot, j, :, 3 * half:4 * half], yr2.at[k, j], r2r.at[k, j], ydev)
        elif j == 1:
            reuse(("x2",), k)
            product(k, j, 1)
            product(k, j, 2)
            put(("x2",), k, part.at[slot, 1, :, half:3 * half], xr2.at[k], r2r.at[k, 2], xdev)
            product(k, j, 0)
        else:
            for i in (2, 0, 1):
                product(k, j, i)

    def reduce2x(k):
        slot = k % slots
        reuse(("x3",), k)
        arrived(yr2.at[k, 1], r2r.at[k, 1])
        x3s[slot] = (part[slot, 1, :, 0:half].astype(F32) + yr2[k, 1].astype(F32)).astype(BF16)
        put(("x3",), k, x3s.at[slot], x3r.at[k], r3r.at[k, 0], xdev)

    def reduce2y(k):
        slot = k % slots
        reuse(("y3",), k)
        arrived(xr2.at[k], r2r.at[k, 2])
        y3s[slot] = (part[slot, 0, :, 2 * half:3 * half].astype(F32) + xr2[k, :, half:cols].astype(F32)).astype(BF16)
        put(("y3",), k, y3s.at[slot], y3r.at[k], r3r.at[k, 1], ydev)

    def finish(k, side, value):
        slot = k % slots
        if k == 0:
            own[side] = value
        else:
            if k > slots:
                reuse(("z4", side), k)
            zsb[slot, side] = value.astype(BF16)
            put(("z4", side), k, zsb.at[slot, side], zr4.at[z, side], z4r.at[z, side], plane_dev(planes[k]))

    def reduce3l(k):
        arrived(yr2.at[k, 0], r2r.at[k, 0])
        arrived(x3r.at[k], r3r.at[k, 0])
        finish(k, 0, part[k % slots, 0, :, 0:half].astype(F32) + yr2[k, 0].astype(F32) + x3r[k].astype(F32))

    def reduce3r(k):
        arrived(y3r.at[k], r3r.at[k, 1])
        finish(k, 1, part[k % slots, 0, :, half:cols].astype(F32) + xr2[k, :, 0:half].astype(F32)
               + y3r[k].astype(F32))

    steps = {"x0": take_x0, "y0": take_y0, "z": take_z, "far": send_far, "xk": take_x, "yk": take_y, "c": take_c,
             "U": up, "D": down, "R2x": reduce2x, "R2y": reduce2y, "R3l": reduce3l, "R3r": reduce3r}
    order_of_steps = schedule(nz, slots)
    far = ("far", 0) in order_of_steps
    for name, *at in order_of_steps:
        steps[name](*at)
    for q in range(1, nz):
        plane = (z + q) % nz
        for side in range(2):
            arrived(zr4.at[plane, side], z4r.at[plane, side])
    for side in range(2):
        total = own[side]
        for q in range(1, nz):
            total = total + zr4[(z + q) % nz, side].astype(F32)
        out_ref[:, side * half:(side + 1) * half] = total.astype(BF16)
    for copy, cond in pending:
        if cond is None:
            copy.wait_send()
        else:
            pl.when(cond)(copy.wait_send)
    assert sites[0] <= snd.shape[0]


def local(tokens, expert_ids, combine_weights, gate_weight, up_weight, down_weight):
    rows, width_all = tokens.shape
    exp_local, _, ff = gate_weight.shape
    n_expert = lax.axis_size("expert")
    n_width = lax.axis_size("width")
    assert n_width == 4 and n_expert % 2 == 0 and rows == LANE and exp_local <= SUB
    nz = n_expert // 2
    cols = width_all // n_width
    half = cols // 2
    deep = exp_local * ff
    resident = n_expert * rows * width_all * 2 <= 12 * 2**20
    slots = nz if resident else 2
    dma = pltpu.SemaphoreType.DMA
    anyspace = pl.BlockSpec(memory_space=pl.ANY)
    vmem = pl.BlockSpec(memory_space=pltpu.VMEM)
    out_shape = [jax.ShapeDtypeStruct((rows, cols), BF16)]
    out_specs = [vmem]
    scratch = [
        pltpu.VMEM((exp_local, width_all, 2 * ff), BF16),
        pltpu.VMEM((2, deep, 2 * cols), BF16),
        pltpu.VMEM((rows, 2 * ff), F32),
        pltpu.VMEM((slots, 2, rows, deep), BF16),
        pltpu.VMEM((nz, 2, rows, deep), BF16),
        pltpu.VMEM((slots, 2, rows, 2 * cols), BF16),
        pltpu.VMEM((nz, 2, rows, half), BF16),
        pltpu.VMEM((nz, rows, cols), BF16),
        pltpu.VMEM((slots, rows, half), BF16),
        pltpu.VMEM((slots, rows, half), BF16),
        pltpu.VMEM((nz, rows, half), BF16),
        pltpu.VMEM((nz, rows, half), BF16),
        pltpu.VMEM((slots, 2, rows, half), BF16),
        pltpu.VMEM((nz, 2, rows, half), BF16),
        pltpu.VMEM((2, rows, half), F32),
        pltpu.VMEM((n_expert, SUB, rows), F32),
        pltpu.VMEM((n_expert, SUB, rows), F32),
        dma((2 * exp_local + 3,)),
        dma,
        dma((40 * nz + 16,)),
        dma((nz,)), dma((nz,)), dma((nz, 2)), dma((nz, 4)), dma((n_expert,)),
        dma((3,)), dma((nz, 2, exp_local)), dma((nz, 3)), dma((nz, 2)), dma((nz, 2)),
    ]
    blocks = (n_expert, rows, width_all)
    if resident:
        scratch.append(pltpu.VMEM(blocks, BF16))
    else:
        out_shape.append(jax.ShapeDtypeStruct(blocks, BF16))
        out_specs.append(anyspace)
        scratch += [pltpu.VMEM((2, 2, rows, width_all), BF16), dma]
    out = pl.pallas_call(
        functools.partial(kernel, nz, resident, slots, exp_local, rows, width_all, ff),
        out_shape=out_shape,
        in_specs=[anyspace, vmem, vmem, anyspace, anyspace, anyspace],
        out_specs=out_specs,
        scratch_shapes=scratch,
        compiler_params=pltpu.CompilerParams(
            collective_id=0, has_side_effects=True, vmem_limit_bytes=66_000_000),
    )(tokens, expert_ids.T, combine_weights.T, gate_weight, up_weight,
      down_weight.reshape(deep, width_all))
    return out[0]


def solution(mesh):
    placed = (
        P("expert", None),
        P("expert", None),
        P("expert", None),
        P("expert", None, "width"),
        P("expert", None, "width"),
        P("expert", "width", None),
    )
    return jax.shard_map(
        local, mesh=mesh, in_specs=placed, out_specs=P("expert", "width"), check_vma=False
    )
```

```python
import functools

import jax
import jax.numpy as jnp
from jax import lax
from jax.experimental import pallas as pl
from jax.experimental.pallas import tpu as pltpu
from jax.sharding import PartitionSpec as P

LANE = 128
SUB = 8
F32 = jnp.float32
BF16 = jnp.bfloat16
MESH = pl.DeviceIdType.MESH


def schedule(nz, parts):
    if nz == 4 and parts == 1:
        return [('x0', 0), ('c', 0, 0), ('z', 1, 0, 1, 0), ('U', 0, 0), ('z', 1, 0, -1, 0), ('z', 1, 1, 1, 0), ('xk', 1, 0), ('z', 1, 1, -1, 0), ('z', 2, 0, 1, 0), ('c', 1, 1), ('z', 2, 0, -1, 0), ('U', 1, 1), ('y0', 0), ('yk', 1, 0), ('D', 1, 1, 0), ('D', 1, 1, 1), ('c', 0, 1), ('D', 0, 0, 0), ('z', 2, 1, -1, 0), ('xk', 2, 0), ('c', 1, 0), ('U', 1, 0), ('z', 3, 0, -1, 0), ('z', 2, 1, 1, 0), ('z', 3, 0, 1, 0), ('yk', 2, 0), ('c', 2, 1), ('U', 2, 1), ('c', 2, 0), ('U', 0, 1), ('D', 2, 1, 0), ('D', 2, 1, 1), ('z', 3, 1, 1, 0), ('R2x', 1), ('D', 1, 0, 0), ('U', 2, 0), ('D', 1, 0, 1), ('R2y', 1), ('xk', 3, 0), ('D', 0, 0, 1), ('D', 2, 0, 0), ('R2x', 2), ('z', 3, 1, -1, 0), ('c', 3, 1), ('U', 3, 1), ('R3l', 1), ('D', 2, 0, 1), ('D', 3, 1, 0), ('yk', 3, 0), ('c', 3, 0), ('D', 3, 1, 1), ('R3r', 1), ('R2y', 2), ('R3l', 2), ('U', 3, 0), ('D', 3, 0, 0), ('R2x', 3), ('R3r', 2), ('D', 0, 1, 0), ('D', 3, 0, 1), ('D', 0, 1, 1), ('R2y', 3), ('R3l', 3), ('R3r', 3), ('R2x', 0), ('R2y', 0), ('R3l', 0), ('R3r', 0)]
    def each(*step):
        return [(*step, h) for h in range(parts)]

    def near(d, j):
        return each("z", d, j, 1) + each("z", d, j, -1) if d < nz else []

    order = [*each("x0"), *near(1, 0), *each("y0"), *near(1, 1)]
    for k in range(nz):
        if k:
            order += each("xk", k) + each("yk", k)
        order += [("c", k, 1), ("U", k, 1), ("c", k, 0), ("U", k, 0), *near(k + 2, 0)]
        if k >= 2:
            order += [("R3l", k - 2), ("R3r", k - 2)]
        order += [("D", k, 1, 0), ("D", k, 1, 1), ("D", k, 0, 0), ("D", k, 0, 1), *near(k + 2, 1)]
        if k >= 1:
            order += [("R2x", k - 1), ("R2y", k - 1)]
    order += [("R2x", nz - 1), ("R2y", nz - 1)]
    for k in range(max(nz - 2, 0), nz):
        order += [("R3l", k), ("R3r", k)]
    return order


def kernel(nz, resident, slots, parts, exp_local, rows, width_all, ff,
           x_ref, ids_ref, wts_ref, g_hbm, u_hbm, d_hbm, out_ref, *rest):
    if resident:
        land, rest = rest[-1], rest[:-1]
        xbuf = lsem = None
    else:
        land, rest = rest[0], rest[1:]
        xbuf, lsem, rest = rest[-2], rest[-1], rest[:-2]
    (wgu, dwv, acc, hid, hidr, part, yr2, xr2, x3s, y3s, x3r, y3r, zsb, zr4, own, cwt, cw,
     wsem, osem, snd, xr, yr, zr, cr, cwr, dwr, hr, r2r, r3r, z4r) = rest

    e, w = lax.axis_index("expert"), lax.axis_index("width")
    z, x = e // 2, e % 2
    y, c = w // 2, w % 2
    s = (x + y) % 2
    n_expert = 2 * nz
    deep = exp_local * ff
    cols = width_all // 4
    half = cols // 2
    quarter = rows // 4
    xdev = (z * 2 + 1 - x, w)
    ydev = (e, (1 - y) * 2 + c)
    cdev = (e, y * 2 + 1 - c)

    def plane_dev(plane):
        return plane * 2 + x, w

    def remote(src, dst, send, recv, dev):
        return pltpu.make_async_remote_copy(
            src_ref=src, dst_ref=dst, send_sem=send, recv_sem=recv,
            device_id=dev, device_id_type=MESH)

    sites = [0]
    pending = []

    def go(src, dst, recv, dev, cond=None, keep=True):
        copy = remote(src, dst, snd.at[sites[0]], recv, dev)
        sites[0] += 1
        if cond is None:
            copy.start()
        else:
            pl.when(cond)(copy.start)
        if keep:
            pending.append((copy, cond))
        return copy

    def arrived(ref, recv):
        remote(ref, ref, snd.at[0], recv, xdev).wait_recv()

    sub = quarter // parts

    def piece(cls, core):
        return [pl.ds(pl.multiple_of((cls * 2 + core) * quarter + h * sub, sub), sub) for h in range(parts)]

    mine, twin = piece(s, c), piece(1 - s, c)
    core_mine, core_twin = piece(s, 1 - c), piece(1 - s, 1 - c)

    def block(plane, j):
        return plane * 2 + (x if j == 0 else 1 - x)

    barrier = pltpu.get_barrier_semaphore()
    for q in range(1, n_expert):
        pl.semaphore_signal(barrier, inc=1, device_id=((e + q) % n_expert, w), device_id_type=MESH)
    for peer in (ydev, cdev):
        pl.semaphore_signal(barrier, inc=1, device_id=peer, device_id_type=MESH)
    weights = []
    for k in range(exp_local):
        for i, ref in enumerate((g_hbm, u_hbm)):
            copy = pltpu.make_async_copy(
                ref.at[k], wgu.at[k, :, i * ff:(i + 1) * ff], wsem.at[2 * k + i])
            copy.start()
            weights.append(copy)

    own_load = pltpu.make_async_copy(x_ref, land.at[e], osem)
    own_load.start()

    def spans(core):
        first = pl.multiple_of((2 * y + core) * cols, LANE)
        second = pl.multiple_of((2 * (1 - y) + core) * cols, LANE)
        return ((pl.ds(first, cols), slice(0, cols)),
                (pl.ds(pl.multiple_of(second + half, LANE), half), slice(cols, cols + half)),
                (pl.ds(second, half), slice(cols + half, 2 * cols)))

    downs = []
    for i, (src, dst) in enumerate(spans(c)):
        copy = pltpu.make_async_copy(d_hbm.at[:, src], dwv.at[0, :, dst], wsem.at[2 * exp_local + i])
        copy.start()
        downs.append(copy)

    tall = (n_expert * SUB, rows)
    line = lax.broadcasted_iota(jnp.int32, tall, 0)
    spot = line % SUB
    name = jnp.where(spot < exp_local, (line // SUB) * exp_local + spot, -1)
    dense = jnp.zeros(tall, F32)
    for k in range(ids_ref.shape[0]):
        dense = dense + jnp.where(ids_ref[k:k + 1, :] == name, wts_ref[k:k + 1, :], 0.0)
    cwt[...] = dense.reshape(n_expert, SUB, rows)

    pl.semaphore_wait(barrier, n_expert + 1)

    for h in range(parts):
        go(x_ref.at[twin[h]], land.at[e, twin[h]], xr.at[z, h], xdev)
    for h in range(parts):
        for sign in (1, -1):
            go(x_ref.at[mine[h]], land.at[e, mine[h]], zr.at[z, 0, h], plane_dev(z + sign),
               (z + sign >= 0) & (z + sign < nz))
    for i, (src, dst) in enumerate(spans(1 - c)):
        go(d_hbm.at[:, src], dwv.at[1, :, dst], dwr.at[i], cdev)

    for q in range(1, n_expert):
        to = (e + q) % n_expert
        go(cwt.at[to], cw.at[e], cwr.at[e], (to, w))
    cw[e] = cwt[e]

    def order(k):
        if k == 0:
            return z
        short = jnp.minimum(z, nz - 1 - z)
        way = jnp.where(2 * z < nz - 1, 1, -1)
        near = (k + 1) // 2 if k % 2 else -(k // 2)
        return z + way * jnp.where(k <= 2 * short, near, k - short)

    planes = [order(k) for k in range(nz)]

    def take_x0(h):
        ref = land.at[block(z, 1), mine[h]]
        arrived(ref, xr.at[z, h])
        for sign in (1, -1):
            go(ref, ref, zr.at[z, 1, h], plane_dev(z + sign), (z + sign >= 0) & (z + sign < nz))
        go(ref, ref, yr.at[z, h], ydev)
        go(ref, ref, cr.at[z, 1, h], cdev)

    def take_y0(h):
        ref = land.at[block(z, 1), twin[h]]
        arrived(ref, yr.at[z, h])
        go(ref, ref, cr.at[z, 3, h], cdev)

    def take_z(d, j, side, h):
        sign = side * jnp.where(2 * z < nz - 1, 1, -1)
        plane, onward = z + sign * d, z - sign
        here = (plane >= 0) & (plane < nz)
        further = here & (onward >= 0) & (onward < nz)
        ref = land.at[block(plane, j), mine[h]]

        @pl.when(here)
        def _():
            arrived(ref, zr.at[plane, j, h])

        if d < nz - 1:
            go(ref, ref, zr.at[plane, j, h], plane_dev(onward), further)
        if j == 0:
            go(ref, ref, xr.at[plane, h], xdev, here)
            go(ref, ref, yr.at[plane, h], ydev, here)
        go(ref, ref, cr.at[plane, j, h], cdev, here)

    def take_x(k, h):
        plane = planes[k]
        ref = land.at[block(plane, 1), twin[h]]
        arrived(ref, xr.at[plane, h])
        go(ref, ref, cr.at[plane, 3, h], cdev)

    def take_y(k, h):
        plane = planes[k]
        ref = land.at[block(plane, 0), twin[h]]
        arrived(ref, yr.at[plane, h])
        go(ref, ref, cr.at[plane, 2, h], cdev)

    def take_c(k, j):
        whole = block(planes[k], j)
        if k == 0 and j == 0:
            own_load.wait()
        else:
            for i in (j, j + 2):
                for h in range(parts):
                    arrived(land.at[whole, (core_mine if i < 2 else core_twin)[h]], cr.at[planes[k], i, h])
            arrived(cw.at[whole], cwr.at[whole])
        if not resident:
            copy = pltpu.make_async_copy(land.at[whole], xbuf.at[k % 2, j], lsem)
            copy.start()
            copy.wait()

    sent = {}

    def put(key, k, src, dst, recv, dev):
        sent[key + (k,)] = go(src, dst, recv, dev, keep=k >= nz - slots)

    def reuse(key, k):
        if k >= slots:
            sent[key + (k - slots,)].wait_send()

    tile = 256
    first = []

    def up(k, j):
        if not first:
            for copy in weights:
                copy.wait()
            first.append(k)
        slot = k % slots
        tokens = (land.at[block(planes[k], j)] if resident else xbuf.at[k % 2, j])
        square = (rows, rows)
        eye = lax.broadcasted_iota(jnp.int32, square, 0) == lax.broadcasted_iota(jnp.int32, square, 1)
        for i in range(exp_local):
            def gate_up(at):
                acc[:, at] = jnp.dot(tokens[...], wgu[i, :, at], preferred_element_type=F32)

            if resident:
                for t in range(2 * ff // tile):
                    gate_up(slice(t * tile, (t + 1) * tile))
            else:
                @pl.loop(0, 2 * ff // tile)
                def _(t):
                    gate_up(pl.ds(pl.multiple_of(t * tile, LANE), tile))

            row = cw[block(planes[k], j), i:i + 1, :]
            scale = jnp.sum(jnp.where(eye, jnp.broadcast_to(row, square), 0.0), axis=1, keepdims=True)
            at = slice(i * ff, (i + 1) * ff)
            reuse(("h", j, i), k)
            hid[slot, j, :, at] = (jax.nn.silu(acc[:, 0:ff]) * acc[:, ff:2 * ff] * scale).astype(BF16)
            put(("h", j, i), k, hid.at[slot, j, :, at], hidr.at[k, j, :, at], hr.at[k, j, i], cdev)

    ready = []

    def product(k, j, i):
        at = slice(i * half, (i + 1) * half)
        value = (jnp.dot(hid[k % slots, j], dwv[0, :, at], preferred_element_type=F32)
                 + jnp.dot(hidr[k, j], dwv[1, :, at], preferred_element_type=F32))
        part[k % slots, j, :, at] = value.astype(BF16)

    def down(k, j, step):
        slot = k % slots
        if step == 0:
            if not ready:
                for copy in downs:
                    copy.wait()
                for i, (_, dst) in enumerate(spans(c)):
                    arrived(dwv.at[1, :, dst], dwr.at[i])
                ready.append(k)
            for i in range(exp_local):
                at = slice(i * ff, (i + 1) * ff)
                arrived(hidr.at[k, j, :, at], hr.at[k, j, i])
            reuse(("y2", j), k)
            product(k, j, 3)
            put(("y2", j), k, part.at[slot, j, :, 3 * half:4 * half], yr2.at[k, j], r2r.at[k, j], ydev)
        elif j == 1:
            reuse(("x2",), k)
            product(k, j, 1)
            product(k, j, 2)
            put(("x2",), k, part.at[slot, 1, :, half:3 * half], xr2.at[k], r2r.at[k, 2], xdev)
            product(k, j, 0)
        else:
            for i in (2, 0, 1):
                product(k, j, i)

    def reduce2x(k):
        slot = k % slots
        reuse(("x3",), k)
        arrived(yr2.at[k, 1], r2r.at[k, 1])
        x3s[slot] = (part[slot, 1, :, 0:half].astype(F32) + yr2[k, 1].astype(F32)).astype(BF16)
        put(("x3",), k, x3s.at[slot], x3r.at[k], r3r.at[k, 0], xdev)

    def reduce2y(k):
        slot = k % slots
        reuse(("y3",), k)
        arrived(xr2.at[k], r2r.at[k, 2])
        y3s[slot] = (part[slot, 0, :, 2 * half:3 * half].astype(F32) + xr2[k, :, half:cols].astype(F32)).astype(BF16)
        put(("y3",), k, y3s.at[slot], y3r.at[k], r3r.at[k, 1], ydev)

    def finish(k, side, value):
        slot = k % slots
        if k == 0:
            own[side] = value
        else:
            if k > slots:
                reuse(("z4", side), k)
            zsb[slot, side] = value.astype(BF16)
            put(("z4", side), k, zsb.at[slot, side], zr4.at[z, side], z4r.at[z, side], plane_dev(planes[k]))

    def reduce3l(k):
        arrived(yr2.at[k, 0], r2r.at[k, 0])
        arrived(x3r.at[k], r3r.at[k, 0])
        finish(k, 0, part[k % slots, 0, :, 0:half].astype(F32) + yr2[k, 0].astype(F32) + x3r[k].astype(F32))

    def reduce3r(k):
        arrived(y3r.at[k], r3r.at[k, 1])
        finish(k, 1, part[k % slots, 0, :, half:cols].astype(F32) + xr2[k, :, 0:half].astype(F32)
               + y3r[k].astype(F32))

    steps = {"x0": take_x0, "y0": take_y0, "z": take_z, "xk": take_x, "yk": take_y, "c": take_c,
             "U": up, "D": down, "R2x": reduce2x, "R2y": reduce2y, "R3l": reduce3l, "R3r": reduce3r}
    for name, *at in schedule(nz, parts):
        steps[name](*at)
    for q in range(1, nz):
        plane = (z + q) % nz
        for side in range(2):
            arrived(zr4.at[plane, side], z4r.at[plane, side])
    for side in range(2):
        total = own[side]
        for q in range(1, nz):
            total = total + zr4[(z + q) % nz, side].astype(F32)
        out_ref[:, side * half:(side + 1) * half] = total.astype(BF16)
    for copy, cond in pending:
        if cond is None:
            copy.wait_send()
        else:
            pl.when(cond)(copy.wait_send)
    assert sites[0] <= snd.shape[0]


def local(tokens, expert_ids, combine_weights, gate_weight, up_weight, down_weight):
    rows, width_all = tokens.shape
    exp_local, _, ff = gate_weight.shape
    n_expert = lax.axis_size("expert")
    n_width = lax.axis_size("width")
    assert n_width == 4 and n_expert % 2 == 0 and rows == LANE and exp_local <= SUB
    nz = n_expert // 2
    cols = width_all // n_width
    half = cols // 2
    deep = exp_local * ff
    resident = n_expert * rows * width_all * 2 <= 12 * 2**20
    slots = nz if resident else 2
    parts = 1
    dma = pltpu.SemaphoreType.DMA
    anyspace = pl.BlockSpec(memory_space=pl.ANY)
    vmem = pl.BlockSpec(memory_space=pltpu.VMEM)
    out_shape = [jax.ShapeDtypeStruct((rows, cols), BF16)]
    out_specs = [vmem]
    scratch = [
        pltpu.VMEM((exp_local, width_all, 2 * ff), BF16),
        pltpu.VMEM((2, deep, 2 * cols), BF16),
        pltpu.VMEM((rows, 2 * ff), F32),
        pltpu.VMEM((slots, 2, rows, deep), BF16),
        pltpu.VMEM((nz, 2, rows, deep), BF16),
        pltpu.VMEM((slots, 2, rows, 2 * cols), BF16),
        pltpu.VMEM((nz, 2, rows, half), BF16),
        pltpu.VMEM((nz, rows, cols), BF16),
        pltpu.VMEM((slots, rows, half), BF16),
        pltpu.VMEM((slots, rows, half), BF16),
        pltpu.VMEM((nz, rows, half), BF16),
        pltpu.VMEM((nz, rows, half), BF16),
        pltpu.VMEM((slots, 2, rows, half), BF16),
        pltpu.VMEM((nz, 2, rows, half), BF16),
        pltpu.VMEM((2, rows, half), F32),
        pltpu.VMEM((n_expert, SUB, rows), F32),
        pltpu.VMEM((n_expert, SUB, rows), F32),
        dma((2 * exp_local + 3,)),
        dma,
        dma((40 * parts * nz + 16,)),
        dma((nz, parts)), dma((nz, parts)), dma((nz, 2, parts)), dma((nz, 4, parts)), dma((n_expert,)),
        dma((3,)), dma((nz, 2, exp_local)), dma((nz, 3)), dma((nz, 2)), dma((nz, 2)),
    ]
    blocks = (n_expert, rows, width_all)
    if resident:
        scratch.append(pltpu.VMEM(blocks, BF16))
    else:
        out_shape.append(jax.ShapeDtypeStruct(blocks, BF16))
        out_specs.append(anyspace)
        scratch += [pltpu.VMEM((2, 2, rows, width_all), BF16), dma]
    out = pl.pallas_call(
        functools.partial(kernel, nz, resident, slots, parts, exp_local, rows, width_all, ff),
        out_shape=out_shape,
        in_specs=[anyspace, vmem, vmem, anyspace, anyspace, anyspace],
        out_specs=out_specs,
        scratch_shapes=scratch,
        compiler_params=pltpu.CompilerParams(
            collective_id=0, has_side_effects=True, vmem_limit_bytes=66_000_000),
    )(tokens, expert_ids.T, combine_weights.T, gate_weight, up_weight,
      down_weight.reshape(deep, width_all))
    return out[0]


def solution(mesh):
    placed = (
        P("expert", None),
        P("expert", None),
        P("expert", None),
        P("expert", None, "width"),
        P("expert", None, "width"),
        P("expert", "width", None),
    )
    return jax.shard_map(
        local, mesh=mesh, in_specs=placed, out_specs=P("expert", "width"), check_vma=False
    )
```

```python
import functools

import jax
import jax.numpy as jnp
from jax import lax
from jax.experimental import pallas as pl
from jax.experimental.pallas import tpu as pltpu
from jax.sharding import PartitionSpec as P

LANE = 128
SUB = 8
F32 = jnp.float32
BF16 = jnp.bfloat16
MESH = pl.DeviceIdType.MESH


def schedule(nz, parts):
    if nz == 4 and parts == 1:
        return [('x0', 0), ('c', 0, 0), ('z', 1, 0, 1, 0), ('U', 0, 0), ('z', 1, 0, -1, 0), ('z', 1, 1, 1, 0), ('xk', 1, 0), ('z', 1, 1, -1, 0), ('z', 2, 0, 1, 0), ('c', 1, 1), ('z', 2, 0, -1, 0), ('U', 1, 1), ('y0', 0), ('yk', 1, 0), ('D', 1, 1, 0), ('D', 1, 1, 1), ('c', 0, 1), ('D', 0, 0, 0), ('z', 2, 1, -1, 0), ('xk', 2, 0), ('c', 1, 0), ('U', 1, 0), ('z', 3, 0, -1, 0), ('z', 2, 1, 1, 0), ('z', 3, 0, 1, 0), ('yk', 2, 0), ('c', 2, 1), ('U', 2, 1), ('c', 2, 0), ('U', 0, 1), ('D', 2, 1, 0), ('D', 2, 1, 1), ('z', 3, 1, 1, 0), ('R2x', 1), ('D', 1, 0, 0), ('U', 2, 0), ('D', 1, 0, 1), ('R2y', 1), ('xk', 3, 0), ('D', 0, 0, 1), ('D', 2, 0, 0), ('R2x', 2), ('z', 3, 1, -1, 0), ('c', 3, 1), ('U', 3, 1), ('R3l', 1), ('D', 2, 0, 1), ('D', 3, 1, 0), ('yk', 3, 0), ('c', 3, 0), ('D', 3, 1, 1), ('R3r', 1), ('R2y', 2), ('R3l', 2), ('U', 3, 0), ('D', 3, 0, 0), ('R2x', 3), ('R3r', 2), ('D', 0, 1, 0), ('D', 3, 0, 1), ('D', 0, 1, 1), ('R2y', 3), ('R3l', 3), ('R3r', 3), ('R2x', 0), ('R2y', 0), ('R3l', 0), ('R3r', 0)]
    def each(*step):
        return [(*step, h) for h in range(parts)]

    def near(d, j):
        return each("z", d, j, 1) + each("z", d, j, -1) if d < nz else []

    order = [*each("x0"), *near(1, 0), *each("y0"), *near(1, 1)]
    for k in range(nz):
        if k:
            order += each("xk", k) + each("yk", k)
        order += [("c", k, 1), ("U", k, 1), ("c", k, 0), ("U", k, 0), *near(k + 2, 0)]
        if k >= 2:
            order += [("R3l", k - 2), ("R3r", k - 2)]
        order += [("D", k, 1, 0), ("D", k, 1, 1), ("D", k, 0, 0), ("D", k, 0, 1), *near(k + 2, 1)]
        if k >= 1:
            order += [("R2x", k - 1), ("R2y", k - 1)]
    order += [("R2x", nz - 1), ("R2y", nz - 1)]
    for k in range(max(nz - 2, 0), nz):
        order += [("R3l", k), ("R3r", k)]
    return order


def kernel(nz, resident, slots, parts, exp_local, rows, width_all, ff,
           x_ref, ids_ref, wts_ref, g_hbm, u_hbm, d_hbm, out_ref, *rest):
    if resident:
        land, rest = rest[-1], rest[:-1]
        xbuf = lsem = None
    else:
        land, rest = rest[0], rest[1:]
        xbuf, lsem, rest = rest[-2], rest[-1], rest[:-2]
    (wgu, dwv, acc, hid, hidr, part, yr2, xr2, x3s, y3s, x3r, y3r, zsb, zr4, own, cwt, cw,
     wsem, osem, snd, xr, yr, zr, cr, cwr, dwr, hr, r2r, r3r, z4r) = rest

    e, w = lax.axis_index("expert"), lax.axis_index("width")
    z, x = e // 2, e % 2
    y, c = w // 2, w % 2
    s = (x + y) % 2
    n_expert = 2 * nz
    deep = exp_local * ff
    cols = width_all // 4
    half = cols // 2
    quarter = rows // 4
    xdev = (z * 2 + 1 - x, w)
    ydev = (e, (1 - y) * 2 + c)
    cdev = (e, y * 2 + 1 - c)

    def plane_dev(plane):
        return plane * 2 + x, w

    def remote(src, dst, send, recv, dev):
        return pltpu.make_async_remote_copy(
            src_ref=src, dst_ref=dst, send_sem=send, recv_sem=recv,
            device_id=dev, device_id_type=MESH)

    sites = [0]
    pending = []

    def go(src, dst, recv, dev, cond=None, keep=True):
        copy = remote(src, dst, snd.at[sites[0]], recv, dev)
        sites[0] += 1
        if cond is None:
            copy.start()
        else:
            pl.when(cond)(copy.start)
        if keep:
            pending.append((copy, cond))
        return copy

    def arrived(ref, recv):
        remote(ref, ref, snd.at[0], recv, xdev).wait_recv()

    sub = quarter // parts

    def piece(cls, core):
        return [pl.ds(pl.multiple_of((cls * 2 + core) * quarter + h * sub, sub), sub) for h in range(parts)]

    mine, twin = piece(s, c), piece(1 - s, c)
    core_mine, core_twin = piece(s, 1 - c), piece(1 - s, 1 - c)

    def block(plane, j):
        return plane * 2 + (x if j == 0 else 1 - x)

    barrier = pltpu.get_barrier_semaphore()
    for q in range(1, n_expert):
        pl.semaphore_signal(barrier, inc=1, device_id=((e + q) % n_expert, w), device_id_type=MESH)
    for peer in (ydev, cdev):
        pl.semaphore_signal(barrier, inc=1, device_id=peer, device_id_type=MESH)
    weights = []
    for k in range(exp_local):
        for i, ref in enumerate((g_hbm, u_hbm)):
            copy = pltpu.make_async_copy(
                ref.at[k], wgu.at[k, :, i * ff:(i + 1) * ff], wsem.at[2 * k + i])
            copy.start()
            weights.append(copy)

    own_load = pltpu.make_async_copy(x_ref, land.at[e], osem)
    own_load.start()

    def spans(core):
        first = pl.multiple_of((2 * y + core) * cols, LANE)
        second = pl.multiple_of((2 * (1 - y) + core) * cols, LANE)
        return ((pl.ds(first, cols), slice(0, cols)),
                (pl.ds(pl.multiple_of(second + half, LANE), half), slice(cols, cols + half)),
                (pl.ds(second, half), slice(cols + half, 2 * cols)))

    downs = []
    for i, (src, dst) in enumerate(spans(c)):
        copy = pltpu.make_async_copy(d_hbm.at[:, src], dwv.at[0, :, dst], wsem.at[2 * exp_local + i])
        copy.start()
        downs.append(copy)

    tall = (n_expert * SUB, rows)
    line = lax.broadcasted_iota(jnp.int32, tall, 0)
    spot = line % SUB
    name = jnp.where(spot < exp_local, (line // SUB) * exp_local + spot, -1)
    dense = jnp.zeros(tall, F32)
    for k in range(ids_ref.shape[0]):
        dense = dense + jnp.where(ids_ref[k:k + 1, :] == name, wts_ref[k:k + 1, :], 0.0)
    cwt[...] = dense.reshape(n_expert, SUB, rows)

    pl.semaphore_wait(barrier, n_expert + 1)

    for h in range(parts):
        go(x_ref.at[twin[h]], land.at[e, twin[h]], xr.at[z, h], xdev)
    for h in range(parts):
        for sign in (1, -1):
            go(x_ref.at[mine[h]], land.at[e, mine[h]], zr.at[z, 0, h], plane_dev(z + sign),
               (z + sign >= 0) & (z + sign < nz))
    for i, (src, dst) in enumerate(spans(1 - c)):
        go(d_hbm.at[:, src], dwv.at[1, :, dst], dwr.at[i], cdev)

    for q in range(1, n_expert):
        to = (e + q) % n_expert
        go(cwt.at[to], cw.at[e], cwr.at[e], (to, w))
    cw[e] = cwt[e]

    def order(k):
        if k == 0:
            return z
        short = jnp.minimum(z, nz - 1 - z)
        way = jnp.where(2 * z < nz - 1, 1, -1)
        near = (k + 1) // 2 if k % 2 else -(k // 2)
        return z + way * jnp.where(k <= 2 * short, near, k - short)

    planes = [order(k) for k in range(nz)]

    def take_x0(h):
        ref = land.at[block(z, 1), mine[h]]
        arrived(ref, xr.at[z, h])
        for sign in (1, -1):
            go(ref, ref, zr.at[z, 1, h], plane_dev(z + sign), (z + sign >= 0) & (z + sign < nz))
        go(ref, ref, yr.at[z, h], ydev)
        go(ref, ref, cr.at[z, 1, h], cdev)

    def take_y0(h):
        ref = land.at[block(z, 1), twin[h]]
        arrived(ref, yr.at[z, h])
        go(ref, ref, cr.at[z, 3, h], cdev)

    def take_z(d, j, side, h):
        sign = side * jnp.where(2 * z < nz - 1, 1, -1)
        plane, onward = z + sign * d, z - sign
        here = (plane >= 0) & (plane < nz)
        further = here & (onward >= 0) & (onward < nz)
        ref = land.at[block(plane, j), mine[h]]

        @pl.when(here)
        def _():
            arrived(ref, zr.at[plane, j, h])

        if d < nz - 1:
            go(ref, ref, zr.at[plane, j, h], plane_dev(onward), further)
        if j == 0:
            go(ref, ref, xr.at[plane, h], xdev, here)
            go(ref, ref, yr.at[plane, h], ydev, here)
        go(ref, ref, cr.at[plane, j, h], cdev, here)

    def take_x(k, h):
        plane = planes[k]
        ref = land.at[block(plane, 1), twin[h]]
        arrived(ref, xr.at[plane, h])
        go(ref, ref, cr.at[plane, 3, h], cdev)

    def take_y(k, h):
        plane = planes[k]
        ref = land.at[block(plane, 0), twin[h]]
        arrived(ref, yr.at[plane, h])
        go(ref, ref, cr.at[plane, 2, h], cdev)

    def take_c(k, j):
        whole = block(planes[k], j)
        if k == 0 and j == 0:
            own_load.wait()
        else:
            for i in (j, j + 2):
                for h in range(parts):
                    arrived(land.at[whole, (core_mine if i < 2 else core_twin)[h]], cr.at[planes[k], i, h])
            arrived(cw.at[whole], cwr.at[whole])
        if not resident:
            copy = pltpu.make_async_copy(land.at[whole], xbuf.at[k % 2, j], lsem)
            copy.start()
            copy.wait()

    sent = {}

    def put(key, k, src, dst, recv, dev):
        sent[key + (k,)] = go(src, dst, recv, dev, keep=k >= nz - slots)

    def reuse(key, k):
        if k >= slots:
            sent[key + (k - slots,)].wait_send()

    tile = 256
    first = []

    def up(k, j):
        if not first:
            for copy in weights:
                copy.wait()
            first.append(k)
        slot = k % slots
        tokens = (land.at[block(planes[k], j)] if resident else xbuf.at[k % 2, j])
        square = (rows, rows)
        eye = lax.broadcasted_iota(jnp.int32, square, 0) == lax.broadcasted_iota(jnp.int32, square, 1)
        for i in range(exp_local):
            def gate_up(at):
                acc[:, at] = jnp.dot(tokens[...], wgu[i, :, at], preferred_element_type=F32)

            if resident:
                for t in range(2 * ff // tile):
                    gate_up(slice(t * tile, (t + 1) * tile))
            else:
                @pl.loop(0, 2 * ff // tile)
                def _(t):
                    gate_up(pl.ds(pl.multiple_of(t * tile, LANE), tile))

            row = cw[block(planes[k], j), i:i + 1, :]
            scale = jnp.sum(jnp.where(eye, jnp.broadcast_to(row, square), 0.0), axis=1, keepdims=True)
            at = slice(i * ff, (i + 1) * ff)
            reuse(("h", j, i), k)
            hid[slot, j, :, at] = (jax.nn.silu(acc[:, 0:ff]) * acc[:, ff:2 * ff] * scale).astype(BF16)
            put(("h", j, i), k, hid.at[slot, j, :, at], hidr.at[k, j, :, at], hr.at[k, j, i], cdev)

    ready = []

    def product(k, j, i):
        at = slice(i * half, (i + 1) * half)
        value = (jnp.dot(hid[k % slots, j], dwv[0, :, at], preferred_element_type=F32)
                 + jnp.dot(hidr[k, j], dwv[1, :, at], preferred_element_type=F32))
        part[k % slots, j, :, at] = value.astype(BF16)

    def down(k, j, step):
        slot = k % slots
        if step == 0:
            if not ready:
                for copy in downs:
                    copy.wait()
                for i, (_, dst) in enumerate(spans(c)):
                    arrived(dwv.at[1, :, dst], dwr.at[i])
                ready.append(k)
            for i in range(exp_local):
                at = slice(i * ff, (i + 1) * ff)
                arrived(hidr.at[k, j, :, at], hr.at[k, j, i])
            reuse(("y2", j), k)
            product(k, j, 3)
            put(("y2", j), k, part.at[slot, j, :, 3 * half:4 * half], yr2.at[k, j], r2r.at[k, j], ydev)
        elif j == 1:
            reuse(("x2",), k)
            product(k, j, 1)
            product(k, j, 2)
            put(("x2",), k, part.at[slot, 1, :, half:3 * half], xr2.at[k], r2r.at[k, 2], xdev)
            product(k, j, 0)
        else:
            for i in (2, 0, 1):
                product(k, j, i)

    def reduce2x(k):
        slot = k % slots
        reuse(("x3",), k)
        arrived(yr2.at[k, 1], r2r.at[k, 1])
        x3s[slot] = (part[slot, 1, :, 0:half].astype(F32) + yr2[k, 1].astype(F32)).astype(BF16)
        put(("x3",), k, x3s.at[slot], x3r.at[k], r3r.at[k, 0], xdev)

    def reduce2y(k):
        slot = k % slots
        reuse(("y3",), k)
        arrived(xr2.at[k], r2r.at[k, 2])
        y3s[slot] = (part[slot, 0, :, 2 * half:3 * half].astype(F32) + xr2[k, :, half:cols].astype(F32)).astype(BF16)
        put(("y3",), k, y3s.at[slot], y3r.at[k], r3r.at[k, 1], ydev)

    def finish(k, side, value):
        slot = k % slots
        if k == 0:
            own[side] = value
        else:
            if k > slots:
                reuse(("z4", side), k)
            zsb[slot, side] = value.astype(BF16)
            put(("z4", side), k, zsb.at[slot, side], zr4.at[z, side], z4r.at[z, side], plane_dev(planes[k]))

    def reduce3l(k):
        arrived(yr2.at[k, 0], r2r.at[k, 0])
        arrived(x3r.at[k], r3r.at[k, 0])
        finish(k, 0, part[k % slots, 0, :, 0:half].astype(F32) + yr2[k, 0].astype(F32) + x3r[k].astype(F32))

    def reduce3r(k):
        arrived(y3r.at[k], r3r.at[k, 1])
        finish(k, 1, part[k % slots, 0, :, half:cols].astype(F32) + xr2[k, :, 0:half].astype(F32)
               + y3r[k].astype(F32))

    steps = {"x0": take_x0, "y0": take_y0, "z": take_z, "xk": take_x, "yk": take_y, "c": take_c,
             "U": up, "D": down, "R2x": reduce2x, "R2y": reduce2y, "R3l": reduce3l, "R3r": reduce3r}
    def drain(count):
        for copy, cond in pending[:count]:
            if cond is None:
                copy.wait_send()
            else:
                pl.when(cond)(copy.wait_send)
        del pending[:count]

    todo = schedule(nz, parts)
    old = 0
    for i, (name, *at) in enumerate(todo):
        if i == len(todo) - 12:
            old = len(pending)
        if i == len(todo) - 2:
            drain(old)
        steps[name](*at)
    drain(len(pending))
    for q in range(1, nz):
        plane = (z + q) % nz
        for side in range(2):
            arrived(zr4.at[plane, side], z4r.at[plane, side])
    for side in range(2):
        total = own[side]
        for q in range(1, nz):
            total = total + zr4[(z + q) % nz, side].astype(F32)
        out_ref[:, side * half:(side + 1) * half] = total.astype(BF16)
    assert sites[0] <= snd.shape[0]


def local(tokens, expert_ids, combine_weights, gate_weight, up_weight, down_weight):
    rows, width_all = tokens.shape
    exp_local, _, ff = gate_weight.shape
    n_expert = lax.axis_size("expert")
    n_width = lax.axis_size("width")
    assert n_width == 4 and n_expert % 2 == 0 and rows == LANE and exp_local <= SUB
    nz = n_expert // 2
    cols = width_all // n_width
    half = cols // 2
    deep = exp_local * ff
    resident = n_expert * rows * width_all * 2 <= 12 * 2**20
    slots = nz if resident else 2
    parts = 1
    dma = pltpu.SemaphoreType.DMA
    anyspace = pl.BlockSpec(memory_space=pl.ANY)
    vmem = pl.BlockSpec(memory_space=pltpu.VMEM)
    out_shape = [jax.ShapeDtypeStruct((rows, cols), BF16)]
    out_specs = [vmem]
    scratch = [
        pltpu.VMEM((exp_local, width_all, 2 * ff), BF16),
        pltpu.VMEM((2, deep, 2 * cols), BF16),
        pltpu.VMEM((rows, 2 * ff), F32),
        pltpu.VMEM((slots, 2, rows, deep), BF16),
        pltpu.VMEM((nz, 2, rows, deep), BF16),
        pltpu.VMEM((slots, 2, rows, 2 * cols), BF16),
        pltpu.VMEM((nz, 2, rows, half), BF16),
        pltpu.VMEM((nz, rows, cols), BF16),
        pltpu.VMEM((slots, rows, half), BF16),
        pltpu.VMEM((slots, rows, half), BF16),
        pltpu.VMEM((nz, rows, half), BF16),
        pltpu.VMEM((nz, rows, half), BF16),
        pltpu.VMEM((slots, 2, rows, half), BF16),
        pltpu.VMEM((nz, 2, rows, half), BF16),
        pltpu.VMEM((2, rows, half), F32),
        pltpu.VMEM((n_expert, SUB, rows), F32),
        pltpu.VMEM((n_expert, SUB, rows), F32),
        dma((2 * exp_local + 3,)),
        dma,
        dma((40 * parts * nz + 16,)),
        dma((nz, parts)), dma((nz, parts)), dma((nz, 2, parts)), dma((nz, 4, parts)), dma((n_expert,)),
        dma((3,)), dma((nz, 2, exp_local)), dma((nz, 3)), dma((nz, 2)), dma((nz, 2)),
    ]
    blocks = (n_expert, rows, width_all)
    if resident:
        scratch.append(pltpu.VMEM(blocks, BF16))
    else:
        out_shape.append(jax.ShapeDtypeStruct(blocks, BF16))
        out_specs.append(anyspace)
        scratch += [pltpu.VMEM((2, 2, rows, width_all), BF16), dma]
    out = pl.pallas_call(
        functools.partial(kernel, nz, resident, slots, parts, exp_local, rows, width_all, ff),
        out_shape=out_shape,
        in_specs=[anyspace, vmem, vmem, anyspace, anyspace, anyspace],
        out_specs=out_specs,
        scratch_shapes=scratch,
        compiler_params=pltpu.CompilerParams(
            collective_id=0, has_side_effects=True, vmem_limit_bytes=66_000_000),
    )(tokens, expert_ids.T, combine_weights.T, gate_weight, up_weight,
      down_weight.reshape(deep, width_all))
    return out[0]


def solution(mesh):
    placed = (
        P("expert", None),
        P("expert", None),
        P("expert", None),
        P("expert", None, "width"),
        P("expert", None, "width"),
        P("expert", "width", None),
    )
    return jax.shard_map(
        local, mesh=mesh, in_specs=placed, out_specs=P("expert", "width"), check_vma=False
    )
```
